128 devices in a mesh: tok: 16 (over x_lo, z, core), cell: 8 (over y, x_hi).
Axes of the slice: x: 4 (x_hi: 2, x_lo: 2; x = x_hi * 2 + x_lo), y: 4, z: 4, core: 2. Of those that a mesh axis runs over, the one named last changes fastest.
Arguments:
- activations: bfloat16 [16384, 4096], P('tok'), may hold values from -6 to 6
- out_grads: bfloat16 [16384, 1024], P('tok'), may hold values from -6 to 6
- query_ids: int32 [16384], P('tok'), may hold values from 0 to 511
- live: int32 [16], P('tok'), may hold values from 256 to 1024, as said below
- proj_in: bfloat16 [4096, 64], P(None, 'cell'), may hold values from -0.09375 to 0.09375
- proj_out: bfloat16 [1024, 32], replicated, may hold values from -0.1875 to 0.1875
- whitener: bfloat16 [2048, 2048], P('cell')
- stores: bfloat16 [196608, 2048], P(('tok', 'cell')), may hold values from -0.023925781 to 0.023925781
Outputs:
- scores: float32 [512, 196608], P(None, ('tok', 'cell'))
The draws below stay inside these ranges and needn't reach their ends.
Inputs may be any that keep to these rules, and one draw needn't show every extreme that they name: `live`: each entry is a count of valid tokens of one block of 1024; some block is full in every draw.
All inputs are finite; a program needn't handle non-finite values.
Results may differ from the reference program's by a relative error of at most 0.005.
Values may be sent and summed in bfloat16 or wider, within the bound.
No kernel may reach another device: no remote copies, remote signals or barrier semaphores. Data moves between devices by JAX's collectives and lax.ppermute only.
A program may use at most 64 MiB of HBM per device.

```python
import jax
import jax.numpy as jnp

D = 4096
KV = 1024
RA = 64
RB = 32
Q = 512
TOK_DEV = 1024
FEAT = 2048
TOKENS = 16384
STORES = 196608
N_TOK = 16


def draw_live(key, part):
    counts = jax.random.randint(key, (N_TOK,), TOK_DEV // 4, TOK_DEV + 1)
    full_block = jax.random.randint(jax.random.fold_in(key, 7), (), 0, N_TOK)
    return counts.at[full_block].set(TOK_DEV).astype(jnp.int32)


def draw_whitener(key, part):
    diag_key = jax.random.fold_in(key, 11)
    off_key = jax.random.fold_in(key, 13)
    diagonal = jnp.exp(jax.random.uniform(diag_key, (FEAT,), jnp.float32, jnp.log(0.3), jnp.log(3.0)))
    off_part = jax.random.normal(off_key, (FEAT, FEAT), jnp.float32) * (0.6 / FEAT ** 0.5)
    whole = jnp.diag(diagonal) + off_part
    return whole.astype(jnp.bfloat16)


def set_ends(result, own_key, low, largest):
    longest = result.shape.index(max(result.shape))
    spots = []
    for shift in (0, 1):
        where = [jax.random.randint(jax.random.fold_in(own_key, axis), (), 0, length) for axis, length in enumerate(result.shape)]
        where[longest] = (where[longest] + shift) % result.shape[longest]
        spots.append(tuple(where))
    return result.at[spots[0]].set(low).at[spots[1]].set(largest)


def level_of(key, extent, split, least, largest):
    loudness = 1.0
    for axis_at, parts in split:
        steps = jax.random.uniform(jax.random.fold_in(jax.random.fold_in(key, 6), axis_at), (parts,), jnp.float32, least / len(split), largest / len(split))
        loudness = loudness * jnp.repeat(jnp.exp(steps), extent[axis_at] // parts).reshape((-1,) + (1,) * (len(extent) - 1 - axis_at))
    return loudness


def bell_draw(key, dims, width, most, cuts=(), held_as=jnp.bfloat16):
    values = jax.random.normal(key, dims, jnp.float32) * width
    if len(cuts) > 0:
        values = level_of(key, dims, cuts, -0.22, 0.18) * values
    return jnp.clip(values, min=-most, max=most).astype(held_as)


def setup_inputs(seed: int = 0) -> dict:
    key_list = jax.random.split(jax.random.key(seed), 9)
    activations = bell_draw(key_list[0], (TOKENS, D), 1.0, 6.0, ((0, 16),))
    out_grads = bell_draw(key_list[1], (TOKENS, KV), 1.0, 6.0, ((0, 16),))
    query_ids = set_ends(jax.random.randint(key_list[2], (TOKENS,), 0, Q), jax.random.fold_in(key_list[2], 1), 0, Q - 1).astype(jnp.int32)
    live = draw_live(jax.random.fold_in(key_list[8], 71), 0)
    proj_in = bell_draw(key_list[4], (D, RA), D ** -0.5, 0.09375, ((1, 8),))
    proj_out = bell_draw(key_list[5], (KV, RB), KV ** -0.5, 0.1875)
    whitener = draw_whitener(jax.random.fold_in(key_list[8], 71), 0)
    stores = bell_draw(key_list[7], (STORES, FEAT), 0.004, 0.023925781, ((0, 128),))
    return {"activations": activations, "out_grads": out_grads, "query_ids": query_ids, "live": live, "proj_in": proj_in, "proj_out": proj_out, "whitener": whitener, "stores": stores}


def reference(activations, out_grads, query_ids, live, proj_in, proj_out, whitener, stores):
    token_count = activations.shape[0]
    positions = jnp.arange(token_count, dtype=jnp.int32)
    valid_mask = ((positions % TOK_DEV) < live[positions // TOK_DEV]).astype(jnp.float32)
    left_proj = jnp.dot(activations, proj_in, preferred_element_type=jnp.float32)
    right_proj = jnp.dot(out_grads, proj_out, preferred_element_type=jnp.float32)
    outer_cells = (left_proj[:, :, None] * right_proj[:, None, :] * valid_mask[:, None, None])
    outer_cells = outer_cells.reshape(token_count, RA * RB).astype(jnp.bfloat16)
    onehot = (query_ids[:, None] == jnp.arange(Q, dtype=jnp.int32)[None, :]).astype(jnp.bfloat16)
    summed = jnp.dot(onehot.T, outer_cells, preferred_element_type=jnp.float32).astype(jnp.bfloat16)
    whitened = jnp.dot(summed, whitener, preferred_element_type=jnp.float32).astype(jnp.bfloat16)
    return jnp.dot(whitened, stores.T, preferred_element_type=jnp.float32)
```

```python
import jax
import jax.numpy as jnp
from jax import lax
from jax.sharding import PartitionSpec as P

Q = 512
N_X, N_Z, N_CORE = 2, 4, 2
N_TOK = N_X * N_Z * N_CORE
N_Y, N_XH = 4, 2


def tok_of(x, z, core):
    return (x % N_X) * N_Z * N_CORE + (z % N_Z) * N_CORE + core


def cell_of(y, xh):
    return y * N_XH + xh


TOKS = [(x, z, core) for x in range(N_X) for z in range(N_Z) for core in range(N_CORE)]
CELLS = [(y, xh) for y in range(N_Y) for xh in range(N_XH)]

SWAP_X = [(tok_of(x, z, c), tok_of(1 - x, z, c)) for x, z, c in TOKS]
SWAP_CORE = [(tok_of(x, z, c), tok_of(x, z, 1 - c)) for x, z, c in TOKS]
RING_A = [(tok_of(x, z, c), tok_of(x, z + (1 - 2 * c), c)) for x, z, c in TOKS]
RING_B = [(tok_of(x, z, c), tok_of(x, z - (1 - 2 * c), c)) for x, z, c in TOKS]

CELL_ROUNDS = (
    [(cell_of(y, xh), cell_of(y, 1 - xh)) for y, xh in CELLS],
    [(cell_of(y, xh), cell_of(y ^ 1, xh)) for y, xh in CELLS],
    [(cell_of(y, xh), cell_of(N_Y - 1 - y, xh)) for y, xh in CELLS],
)


def shards(activations, out_grads, query_ids, live, proj_in, proj_out, whitener, stores):
    tok_rows = activations.shape[0]
    valid_mask = (jnp.arange(tok_rows, dtype=jnp.int32) < live[0]).astype(jnp.float32)
    left_proj = jnp.dot(activations, proj_in, preferred_element_type=jnp.float32)
    right_proj = jnp.dot(out_grads, proj_out, preferred_element_type=jnp.float32)
    outer_cells = left_proj[:, :, None] * right_proj[:, None, :] * valid_mask[:, None, None]
    outer_cells = outer_cells.reshape(tok_rows, -1).astype(jnp.bfloat16)
    onehot = (query_ids[:, None] == jnp.arange(Q, dtype=jnp.int32)[None, :]).astype(jnp.bfloat16)
    partial_value = lax.dot_general(
        onehot, outer_cells, (((0,), (0,)), ((), ())), preferred_element_type=jnp.float32
    ).astype(jnp.bfloat16)
    pieces = lax.all_to_all(
        partial_value.reshape(N_TOK, Q // N_TOK, -1), "tok", 0, 0, tiled=True
    )
    summed = pieces.astype(jnp.float32).sum(0).astype(jnp.bfloat16)
    total = jnp.dot(summed, whitener, preferred_element_type=jnp.float32)
    for perm in CELL_ROUNDS:
        other = lax.ppermute(total.astype(jnp.bfloat16), "cell", perm)
        total = total + other.astype(jnp.float32)
    own = total.astype(jnp.bfloat16)
    pair = jnp.stack([own, lax.ppermute(own, "tok", SWAP_X)])
    up = lax.ppermute(pair, "tok", RING_A)
    down = lax.ppermute(pair, "tok", RING_B)
    far = lax.ppermute(up, "tok", RING_A)
    half = jnp.stack([pair, up, down, far])
    whole = jnp.stack([half, lax.ppermute(half, "tok", SWAP_CORE)])
    tok = lax.axis_index("tok")
    x, z, core = tok // (N_Z * N_CORE), (tok // N_CORE) % N_Z, tok % N_CORE
    want = jnp.arange(N_TOK, dtype=jnp.int32)
    want_x, want_z, want_core = want // (N_Z * N_CORE), (want // N_CORE) % N_Z, want % N_CORE
    step = (z - want_z) * (1 - 2 * want_core) % N_Z
    slot = jnp.where(step == 2, 3, jnp.where(step == 3, 2, step))
    place = ((want_core != core) * N_Z + slot) * N_X + (want_x != x)
    whitened = whole.reshape(N_TOK, Q // N_TOK, -1)[place].reshape(Q, -1)
    return lax.dot_general(
        whitened, stores, (((1,), (1,)), ((), ())), preferred_element_type=jnp.float32
    )


def solution(mesh):
    in_specs = (
        P("tok", None),
        P("tok", None),
        P("tok"),
        P("tok"),
        P(None, "cell"),
        P(),
        P("cell", None),
        P(("tok", "cell"), None),
    )
    out_specs = P(None, ("tok", "cell"))
    return jax.shard_map(shards, mesh=mesh, in_specs=in_specs, out_specs=out_specs, check_vma=False)
```

```python
import jax
import jax.numpy as jnp
from jax import lax
from jax.experimental import pallas as pl
from jax.experimental.pallas import tpu as pltpu
from jax.sharding import PartitionSpec as P

Q = 512
N_X, N_Z, N_CORE, N_Y, N_XH = 2, 4, 2, 4, 2
N_TOK = N_X * N_Z * N_CORE
BLOCK = Q // N_TOK
AXES = ("tok", "cell")
NT = (((1,), (1,)), ((), ()))


PLACES = [
    (x, z, core, y, xh)
    for x in range(N_X)
    for z in range(N_Z)
    for core in range(N_CORE)
    for y in range(N_Y)
    for xh in range(N_XH)
]


def number(x, z, core, y, xh):
    return (((x * N_Z + z % N_Z) * N_CORE + core) * N_Y + y) * N_XH + xh


def routes(move):
    return [(number(*place), number(*move(*place))) for place in PLACES]


CELL_ROUNDS = (
    routes(lambda x, z, core, y, xh: (1 - x, z, core, y, 1 - xh)),
    routes(lambda x, z, core, y, xh: (x, z, core, y ^ 1, xh)),
    routes(lambda x, z, core, y, xh: (x, z, core, N_Y - 1 - y, xh)),
)
SWAP_X = routes(lambda x, z, core, y, xh: (1 - x, z, core, y, xh))
SWAP_CORE = routes(lambda x, z, core, y, xh: (x, z, 1 - core, y, xh))
RING_A = routes(lambda x, z, core, y, xh: (x, z + 1 - 2 * core, core, y, xh))
RING_B = routes(lambda x, z, core, y, xh: (x, z - 1 + 2 * core, core, y, xh))


def send(value, route):
    return lax.ppermute(value, AXES, route)


def score_slots(slots, stores, out):
    n_rows, width = stores.shape
    step_rows = 512
    steps = n_rows // step_rows
    slot_rows = N_X * N_CORE * BLOCK
    blocks = [piece for _, own, partner in slots for piece in (*own, *partner)]

    def body(*refs):
        piece_refs = refs[: len(blocks)]
        store_ref = refs[len(blocks)]
        out_ref, rows_ref, acc_ref, sems = refs[-4:]
        tok, cell = lax.axis_index("tok"), lax.axis_index("cell")
        core = lax.rem(tok, N_CORE)
        z = lax.rem(lax.div(tok, N_CORE), N_Z)
        x = lax.rem(lax.div(tok, N_CORE * N_Z) + lax.rem(cell, N_XH), N_X)
        for at in range(len(slots)):
            for part in range(4):
                x_at = x if part % 2 == 0 else 1 - x
                core_at = core if part < 2 else 1 - core
                start = pl.multiple_of(at * slot_rows + (x_at * N_CORE + core_at) * BLOCK, BLOCK)
                rows_ref[pl.ds(start, BLOCK), :] = piece_refs[at * 4 + part][...]
        copies = []
        for step in range(steps):
            cols = pl.ds(step * step_rows, step_rows)
            acc = lax.dot_general(
                rows_ref[...], store_ref[cols, :], NT, preferred_element_type=jnp.float32
            )
            acc_ref[:, :, :, :, cols] = acc.reshape(len(slots), N_X, N_CORE, BLOCK, step_rows)
            for at, (distance, _, _) in enumerate(slots):
                z_at = lax.rem(z + distance * (1 - 2 * core) + N_Z, N_Z)
                copy = pltpu.make_async_copy(
                    acc_ref.at[at, :, :, :, cols], out_ref.at[:, z_at, :, :, cols], sems.at[step, at]
                )
                copy.start()
                copies.append(copy)
        for copy in copies:
            copy.wait()

    vmem = pl.BlockSpec(memory_space=pltpu.VMEM)
    hbm = pl.BlockSpec(memory_space=pl.ANY)
    args = [*blocks, stores]
    specs = [vmem] * len(args)
    if out is not None:
        args.append(out)
        specs.append(hbm)
    return pl.pallas_call(
        body,
        in_specs=specs,
        out_specs=hbm,
        out_shape=jax.ShapeDtypeStruct((N_X, N_Z, N_CORE, BLOCK, n_rows), jnp.float32),
        scratch_shapes=[
            pltpu.VMEM((len(slots) * slot_rows, width), jnp.bfloat16),
            pltpu.VMEM((len(slots), N_X, N_CORE, BLOCK, n_rows), jnp.float32),
            pltpu.SemaphoreType.DMA((steps, len(slots))),
        ],
        compiler_params=pltpu.CompilerParams(vmem_limit_bytes=24 << 20),
        input_output_aliases={} if out is None else {len(args) - 1: 0},
    )(*args)


def shards(activations, out_grads, query_ids, live, proj_in, proj_out, whitener, stores):
    tok_rows = activations.shape[0]
    valid_mask = (jnp.arange(tok_rows, dtype=jnp.int32) < live[0]).astype(jnp.float32)
    left_proj = jnp.dot(activations, proj_in, preferred_element_type=jnp.float32)
    right_proj = jnp.dot(out_grads, proj_out, preferred_element_type=jnp.float32)
    outer_cells = left_proj[:, :, None] * right_proj[:, None, :] * valid_mask[:, None, None]
    outer_cells = outer_cells.reshape(tok_rows, -1).astype(jnp.bfloat16)
    swap = (lax.axis_index("cell") % N_XH) * (Q // N_X)
    row_ids = jnp.arange(Q, dtype=jnp.int32) ^ swap
    onehot = (query_ids[:, None] == row_ids[None, :]).astype(jnp.bfloat16)
    partial_value = lax.dot_general(
        onehot, outer_cells, (((0,), (0,)), ((), ())), preferred_element_type=jnp.float32
    ).astype(jnp.bfloat16)
    pieces = lax.all_to_all(partial_value.reshape(N_TOK, BLOCK, -1), "tok", 0, 0, tiled=True)
    summed = pieces.astype(jnp.float32).sum(0).astype(jnp.bfloat16)
    total = jnp.dot(summed, whitener, preferred_element_type=jnp.float32)
    for route in CELL_ROUNDS:
        total = total + send(total.astype(jnp.bfloat16), route).astype(jnp.float32)
    own = total.astype(jnp.bfloat16)
    other = send(own, SWAP_X)
    here = (own, other)
    up = tuple(send(piece, RING_A) for piece in here)
    down = tuple(send(piece, RING_B) for piece in here)
    far = tuple(send(piece, RING_A) for piece in up)
    over = lambda pair: tuple(send(piece, SWAP_CORE) for piece in pair)
    slots = ((0, here, over(here)), (-1, up, over(down)), (1, down, over(up)))
    scores = score_slots(slots, stores, None)
    scores = score_slots(((2, far, over(far)),), stores, scores)
    return scores.reshape(Q, -1)


def solution(mesh):
    in_specs = (
        P("tok", None),
        P("tok", None),
        P("tok"),
        P("tok"),
        P(None, "cell"),
        P(),
        P("cell", None),
        P(("tok", "cell"), None),
    )
    out_specs = P(None, ("tok", "cell"))
    return jax.shard_map(shards, mesh=mesh, in_specs=in_specs, out_specs=out_specs, check_vma=False)
```

```python
import jax
import jax.numpy as jnp
from jax import lax
from jax.experimental import pallas as pl
from jax.experimental.pallas import tpu as pltpu
from jax.sharding import PartitionSpec as P

Q = 512
N_X, N_Z, N_CORE, N_Y, N_XH = 2, 4, 2, 4, 2
N_TOK = N_X * N_Z * N_CORE
BLOCK = Q // N_TOK
AXES = ("tok", "cell")
NT = (((1,), (1,)), ((), ()))


PLACES = [
    (x, z, core, y, xh)
    for x in range(N_X)
    for z in range(N_Z)
    for core in range(N_CORE)
    for y in range(N_Y)
    for xh in range(N_XH)
]


def number(x, z, core, y, xh):
    return (((x * N_Z + z % N_Z) * N_CORE + core) * N_Y + y) * N_XH + xh


def routes(move):
    return [(number(*place), number(*move(*place))) for place in PLACES]


CELL_ROUNDS = (
    routes(lambda x, z, core, y, xh: (1 - x, z, core, y, 1 - xh)),
    routes(lambda x, z, core, y, xh: (x, z, core, y ^ 1, xh)),
    routes(lambda x, z, core, y, xh: (x, z, core, N_Y - 1 - y, xh)),
)
SWAP_X = routes(lambda x, z, core, y, xh: (1 - x, z, core, y, xh))
SWAP_CORE = routes(lambda x, z, core, y, xh: (x, z, 1 - core, y, xh))
RING_A = routes(lambda x, z, core, y, xh: (x, z + 1 - 2 * core, core, y, xh))
RING_B = routes(lambda x, z, core, y, xh: (x, z - 1 + 2 * core, core, y, xh))


def send(value, route):
    return lax.ppermute(value, AXES, route)


def score_blocks(blocks, groups, stores, out):
    n_rows, width = stores.shape
    step_rows = 512
    steps = n_rows // step_rows
    arrays = list({id(block[3]): block[3] for block in blocks}.values())
    number_of = {id(array): at for at, array in enumerate(arrays)}

    def body(*refs):
        array_refs = refs[: len(arrays)]
        store_ref = refs[len(arrays)]
        loads = []
        if out is None:
            out_ref, held_ref, rows_ref, acc_ref, sems, load_sems = refs[-6:]
            for step in range(steps):
                rows = pl.ds(step * step_rows, step_rows)
                load = pltpu.make_async_copy(store_ref.at[rows], held_ref.at[rows], load_sems.at[step])
                load.start()
                loads.append(load)
            store_ref = held_ref
        else:
            out_ref, rows_ref, acc_ref, sems = refs[-4:]
        tok, cell = lax.axis_index("tok"), lax.axis_index("cell")
        core = lax.rem(tok, N_CORE)
        z = lax.rem(lax.div(tok, N_CORE), N_Z)
        x = lax.rem(lax.div(tok, N_CORE * N_Z) + lax.rem(cell, N_XH), N_X)
        up = 1 - 2 * core

        def z_of(distance):
            return lax.rem(z + distance * up + N_Z, N_Z)

        starts = {}
        first = 0
        for group in groups:
            for at in group:
                _, own_x, distance, _, _ = blocks[at]
                x_at = x if own_x else 1 - x
                whole = len(group) > N_X
                place = x_at * N_Z + z_of(distance) if whole else x_at
                starts[at] = first + place * BLOCK
            first += len(group) * BLOCK
        for at, (_, _, _, array, index) in enumerate(blocks):
            start = pl.multiple_of(starts[at], BLOCK)
            rows_ref[pl.ds(start, BLOCK), :] = array_refs[number_of[id(array)]][index]
        copies = []
        for step in range(steps):
            cols = pl.ds(step * step_rows, step_rows)
            if loads:
                loads[step].wait()
            acc = lax.dot_general(
                rows_ref[...], store_ref[cols, :], NT, preferred_element_type=jnp.float32
            )
            acc_ref[:, :, cols] = acc.reshape(len(blocks), BLOCK, step_rows)
            first = 0
            for number_at, group in enumerate(groups):
                own_core, _, distance, _, _ = blocks[group[0]]
                core_at = core if own_core else 1 - core
                size = len(group) // N_X
                for x_at in range(N_X):
                    if size > 1:
                        source = acc_ref.at[pl.ds(first, size), :, cols]
                        target = out_ref.at[x_at, :, core_at, :, cols]
                    else:
                        source = acc_ref.at[first, :, cols]
                        target = out_ref.at[x_at, z_of(distance), core_at, :, cols]
                    first += size
                    copy = pltpu.make_async_copy(source, target, sems.at[step, number_at, x_at])
                    copy.start()
                    copies.append(copy)
        for copy in copies:
            copy.wait()

    vmem = pl.BlockSpec(memory_space=pltpu.VMEM)
    hbm = pl.BlockSpec(memory_space=pl.ANY)
    scores_shape = jax.ShapeDtypeStruct((N_X, N_Z, N_CORE, BLOCK, n_rows), jnp.float32)
    scratch = [
        pltpu.VMEM((len(blocks) * BLOCK, width), jnp.bfloat16),
        pltpu.VMEM((len(blocks), BLOCK, n_rows), jnp.float32),
        pltpu.SemaphoreType.DMA((steps, len(groups), N_X)),
    ]
    params = pltpu.CompilerParams(vmem_limit_bytes=12 << 20)
    if out is None:
        return pl.pallas_call(
            body,
            in_specs=[vmem] * len(arrays) + [pl.BlockSpec(memory_space=pltpu.HBM)],
            out_specs=(hbm, vmem),
            out_shape=(scores_shape, jax.ShapeDtypeStruct(stores.shape, stores.dtype)),
            scratch_shapes=[*scratch, pltpu.SemaphoreType.DMA((steps,))],
            compiler_params=params,
        )(*arrays, stores)
    return pl.pallas_call(
        body,
        in_specs=[vmem] * (len(arrays) + 1) + [hbm],
        out_specs=hbm,
        out_shape=scores_shape,
        scratch_shapes=scratch,
        compiler_params=params,
        input_output_aliases={len(arrays) + 1: 0},
    )(*arrays, stores, out)


def shards(activations, out_grads, query_ids, live, proj_in, proj_out, whitener, stores):
    tok_rows = activations.shape[0]
    valid_mask = (jnp.arange(tok_rows, dtype=jnp.int32) < live[0]).astype(jnp.float32)
    left_proj = jnp.dot(activations, proj_in, preferred_element_type=jnp.float32)
    right_proj = jnp.dot(out_grads, proj_out, preferred_element_type=jnp.float32)
    outer_cells = left_proj[:, :, None] * right_proj[:, None, :] * valid_mask[:, None, None]
    outer_cells = outer_cells.reshape(tok_rows, -1).astype(jnp.bfloat16)
    swap = (lax.axis_index("cell") % N_XH) * (Q // N_X)
    row_ids = jnp.arange(Q, dtype=jnp.int32) ^ swap
    onehot = (query_ids[:, None] == row_ids[None, :]).astype(jnp.bfloat16)
    partial_value = lax.dot_general(
        onehot, outer_cells, (((0,), (0,)), ((), ())), preferred_element_type=jnp.float32
    ).astype(jnp.bfloat16)
    pieces = lax.all_to_all(partial_value.reshape(N_TOK, BLOCK, -1), "tok", 0, 0, tiled=True)
    summed = pieces.astype(jnp.float32).sum(0).astype(jnp.bfloat16)
    total = jnp.dot(summed, whitener, preferred_element_type=jnp.float32)
    for route in CELL_ROUNDS:
        total = total + send(total.astype(jnp.bfloat16), route).astype(jnp.float32)
    own = total.astype(jnp.bfloat16)
    return gather_and_score(own, stores)


def gather_and_score(own, stores):
    here = (own, send(own, SWAP_X))
    up = tuple(send(piece, RING_A) for piece in here)
    down = tuple(send(piece, RING_B) for piece in here)
    far_own = send(up[0], RING_A)
    far_other = send(up[1], RING_A)
    near = jnp.stack([*here, *up, *down])
    near_over = send(near, SWAP_CORE)
    near_at = ((1, 0), (0, 0), (1, -1), (0, -1), (1, 1), (0, 1))
    blocks = [(1, own_x, distance, near, at) for at, (own_x, distance) in enumerate(near_at)]
    scores, held = score_blocks(blocks, ((0, 1), (2, 3), (4, 5)), stores, None)
    far = jnp.stack([far_own, far_other])
    far_over = send(far, SWAP_CORE)
    blocks = [(1, 1, 2, far, 0), (1, 0, 2, far, 1)]
    blocks += [(0, own_x, -distance, near_over, at) for at, (own_x, distance) in enumerate(near_at)]
    blocks += [(0, 1, 2, far_over, 0), (0, 0, 2, far_over, 1)]
    scores = score_blocks(blocks, ((0, 1), tuple(range(2, 10))), held, scores)
    return scores.reshape(Q, -1)


def solution(mesh):
    in_specs = (
        P("tok", None),
        P("tok", None),
        P("tok"),
        P("tok"),
        P(None, "cell"),
        P(),
        P("cell", None),
        P(("tok", "cell"), None),
    )
    out_specs = P(None, ("tok", "cell"))
    return jax.shard_map(shards, mesh=mesh, in_specs=in_specs, out_specs=out_specs, check_vma=False)
```

```python
import jax
import jax.numpy as jnp
from jax import lax
from jax.experimental import pallas as pl
from jax.experimental.pallas import tpu as pltpu
from jax.sharding import PartitionSpec as P

Q = 512
N_X, N_Z, N_CORE, N_Y, N_XH = 2, 4, 2, 4, 2
N_TOK = N_X * N_Z * N_CORE
BLOCK = Q // N_TOK
AXES = ("tok", "cell")
NT = (((1,), (1,)), ((), ()))


PLACES = [
    (x, z, core, y, xh)
    for x in range(N_X)
    for z in range(N_Z)
    for core in range(N_CORE)
    for y in range(N_Y)
    for xh in range(N_XH)
]


def number(x, z, core, y, xh):
    return (((x * N_Z + z % N_Z) * N_CORE + core) * N_Y + y) * N_XH + xh


def routes(move):
    return [(number(*place), number(*move(*place))) for place in PLACES]


SUM_X = routes(lambda x, z, core, y, xh: (1 - x, z, core, y, 1 - xh))
SUM_Y = [
    routes(lambda x, z, core, y, xh, step=step: (x, z, core, (y + step * (1 - 2 * core)) % N_Y, xh)) for step in (1, 3, 2)
]
SWAP_X = routes(lambda x, z, core, y, xh: (1 - x, z, core, y, xh))
SWAP_CORE = routes(lambda x, z, core, y, xh: (x, z, 1 - core, y, xh))
RING_A = routes(lambda x, z, core, y, xh: (x, z + 1 - 2 * core, core, y, xh))
RING_B = routes(lambda x, z, core, y, xh: (x, z - 1 + 2 * core, core, y, xh))


def send(value, route):
    return lax.ppermute(value, AXES, route)


def score_blocks(blocks, groups, stores, out):
    n_rows, width = stores.shape
    step_rows = 512
    steps = n_rows // step_rows
    arrays = list({id(block[3]): block[3] for block in blocks}.values())
    number_of = {id(array): at for at, array in enumerate(arrays)}

    def body(*refs):
        array_refs = refs[: len(arrays)]
        store_ref = refs[len(arrays)]
        out_ref, rows_ref, acc_ref, sems = refs[-4:]
        tok, cell = lax.axis_index("tok"), lax.axis_index("cell")
        core = lax.rem(tok, N_CORE)
        z = lax.rem(lax.div(tok, N_CORE), N_Z)
        x = lax.rem(lax.div(tok, N_CORE * N_Z) + lax.rem(cell, N_XH), N_X)
        up = 1 - 2 * core

        def z_of(distance):
            return lax.rem(z + distance * up + N_Z, N_Z)

        starts = {}
        first = 0
        for group in groups:
            for at in group:
                _, own_x, distance, _, _ = blocks[at]
                x_at = x if own_x else 1 - x
                whole = len(group) > N_X
                place = x_at * N_Z + z_of(distance) if whole else x_at
                starts[at] = first + place * BLOCK
            first += len(group) * BLOCK
        for at, (_, _, _, array, index) in enumerate(blocks):
            start = pl.multiple_of(starts[at], BLOCK)
            rows_ref[pl.ds(start, BLOCK), :] = array_refs[number_of[id(array)]][index]
        copies = []
        for step in range(steps):
            cols = pl.ds(step * step_rows, step_rows)
            acc = lax.dot_general(
                rows_ref[...], store_ref[cols, :], NT, preferred_element_type=jnp.float32
            )
            acc_ref[:, :, cols] = acc.reshape(len(blocks), BLOCK, step_rows)
            first = 0
            for number_at, group in enumerate(groups):
                own_core, _, distance, _, _ = blocks[group[0]]
                core_at = core if own_core else 1 - core
                size = len(group) // N_X
                for x_at in range(N_X):
                    if size > 1:
                        source = acc_ref.at[pl.ds(first, size), :, cols]
                        target = out_ref.at[x_at, :, core_at, :, cols]
                    else:
                        source = acc_ref.at[first, :, cols]
                        target = out_ref.at[x_at, z_of(distance), core_at, :, cols]
                    first += size
                    copy = pltpu.make_async_copy(source, target, sems.at[step, number_at, x_at])
                    copy.start()
                    copies.append(copy)
        for copy in copies:
            copy.wait()

    vmem = pl.BlockSpec(memory_space=pltpu.VMEM)
    hbm = pl.BlockSpec(memory_space=pl.ANY)
    scores_shape = jax.ShapeDtypeStruct((N_X, N_Z, N_CORE, BLOCK, n_rows), jnp.float32)
    scratch = [
        pltpu.VMEM((len(blocks) * BLOCK, width), jnp.bfloat16),
        pltpu.VMEM((len(blocks), BLOCK, n_rows), jnp.float32),
        pltpu.SemaphoreType.DMA((steps, len(groups), N_X)),
    ]
    params = pltpu.CompilerParams(vmem_limit_bytes=12 << 20)
    args = [*arrays, stores]
    specs = [vmem] * len(args)
    if out is not None:
        args.append(out)
        specs.append(hbm)
    return pl.pallas_call(
        body,
        in_specs=specs,
        out_specs=hbm,
        out_shape=scores_shape,
        scratch_shapes=scratch,
        compiler_params=params,
        input_output_aliases={} if out is None else {len(args) - 1: 0},
    )(*args)


def hold(stores):
    parts = 4
    size = stores.shape[0] // parts

    def body(store_ref, held_ref, sems):
        copies = []
        for part in range(parts):
            rows = pl.ds(part * size, size)
            copies.append(pltpu.make_async_copy(store_ref.at[rows], held_ref.at[rows], sems.at[part]))
            copies[-1].start()
        for copy in copies:
            copy.wait()

    return pl.pallas_call(
        body,
        in_specs=[pl.BlockSpec(memory_space=pl.ANY)],
        out_specs=pl.BlockSpec(memory_space=pltpu.VMEM),
        out_shape=jax.ShapeDtypeStruct(stores.shape, stores.dtype),
        scratch_shapes=[pltpu.SemaphoreType.DMA((parts,))],
        compiler_params=pltpu.CompilerParams(vmem_limit_bytes=4 << 20),
    )(pltpu.with_memory_space_constraint(stores, pltpu.HBM))


def shards(activations, out_grads, query_ids, live, proj_in, proj_out, whitener, stores):
    tok_rows = activations.shape[0]
    valid_mask = (jnp.arange(tok_rows, dtype=jnp.int32) < live[0]).astype(jnp.float32)
    left_proj = jnp.dot(activations, proj_in, preferred_element_type=jnp.float32)
    right_proj = jnp.dot(out_grads, proj_out, preferred_element_type=jnp.float32)
    outer_cells = left_proj[:, :, None] * right_proj[:, None, :] * valid_mask[:, None, None]
    outer_cells = outer_cells.reshape(tok_rows, -1).astype(jnp.bfloat16)
    swap = (lax.axis_index("cell") % N_XH) * (Q // N_X)
    row_ids = jnp.arange(Q, dtype=jnp.int32) ^ swap
    onehot = (query_ids[:, None] == row_ids[None, :]).astype(jnp.bfloat16)
    partial_value = lax.dot_general(
        onehot, outer_cells, (((0,), (0,)), ((), ())), preferred_element_type=jnp.float32
    ).astype(jnp.bfloat16)
    pieces = lax.all_to_all(partial_value.reshape(N_TOK, BLOCK, -1), "tok", 0, 0, tiled=True)
    summed = pieces.astype(jnp.float32).sum(0).astype(jnp.bfloat16)
    total = jnp.dot(summed, whitener, preferred_element_type=jnp.float32)
    across = send(total.astype(jnp.bfloat16), SUM_X)
    held = hold(stores)
    total = total + across.astype(jnp.float32)
    rounded = total.astype(jnp.bfloat16)
    for piece in [send(rounded, route) for route in SUM_Y]:
        total = total + piece.astype(jnp.float32)
    return gather_and_score(total.astype(jnp.bfloat16), held)


def gather_and_score(own, held):
    here = (own, send(own, SWAP_X))
    up = tuple(send(piece, RING_A) for piece in here)
    down = tuple(send(piece, RING_B) for piece in here)
    far_own = send(up[0], RING_A)
    far_other = send(up[1], RING_A)
    near = jnp.stack([*here, *up, *down])
    near_over = send(near, SWAP_CORE)
    near_at = ((1, 0), (0, 0), (1, -1), (0, -1), (1, 1), (0, 1))
    blocks = [(1, own_x, distance, near, at) for at, (own_x, distance) in enumerate(near_at)]
    scores = score_blocks(blocks, ((0, 1), (2, 3), (4, 5)), held, None)
    far = jnp.stack([far_own, far_other])
    far_over = send(far, SWAP_CORE)
    blocks = [(1, 1, 2, far, 0), (1, 0, 2, far, 1)]
    blocks += [(0, own_x, -distance, near_over, at) for at, (own_x, distance) in enumerate(near_at)]
    blocks += [(0, 1, 2, far_over, 0), (0, 0, 2, far_over, 1)]
    scores = score_blocks(blocks, ((0, 1), tuple(range(2, 10))), held, scores)
    return scores.reshape(Q, -1)


def solution(mesh):
    in_specs = (
        P("tok", None),
        P("tok", None),
        P("tok"),
        P("tok"),
        P(None, "cell"),
        P(),
        P("cell", None),
        P(("tok", "cell"), None),
    )
    out_specs = P(None, ("tok", "cell"))
    return jax.shard_map(shards, mesh=mesh, in_specs=in_specs, out_specs=out_specs, check_vma=False)
```

```python
import jax
import jax.numpy as jnp
from jax import lax
from jax.experimental import pallas as pl
from jax.experimental.pallas import tpu as pltpu
from jax.sharding import PartitionSpec as P

Q = 512
N_X, N_Z, N_CORE, N_Y, N_XH = 2, 4, 2, 4, 2
N_TOK = N_X * N_Z * N_CORE
BLOCK = Q // N_TOK
AXES = ("tok", "cell")
NT = (((1,), (1,)), ((), ()))
STEP_ROWS = 512


PLACES = [
    (x, z, core, y, xh)
    for x in range(N_X)
    for z in range(N_Z)
    for core in range(N_CORE)
    for y in range(N_Y)
    for xh in range(N_XH)
]


def number(x, z, core, y, xh):
    return (((x * N_Z + z % N_Z) * N_CORE + core) * N_Y + y) * N_XH + xh


def routes(move):
    return [(number(*place), number(*move(*place))) for place in PLACES]


SUM_X = routes(lambda x, z, core, y, xh: (1 - x, z, core, y, 1 - xh))
SUM_Y = [
    routes(lambda x, z, core, y, xh, step=step: (x, z, core, (y + step * (1 - 2 * core)) % N_Y, xh)) for step in (1, 3, 2)
]
SWAP_X = routes(lambda x, z, core, y, xh: (1 - x, z, core, y, xh))
SWAP_CORE = routes(lambda x, z, core, y, xh: (x, z, 1 - core, y, xh))
RING_A = routes(lambda x, z, core, y, xh: (x, z + 1 - 2 * core, core, y, xh))
RING_B = routes(lambda x, z, core, y, xh: (x, z - 1 + 2 * core, core, y, xh))


def send(value, route):
    return lax.ppermute(value, AXES, route)


NEAR_BLOCKS = ((0, 0), (1, 0), (0, -1), (1, -1), (0, 1), (1, 1))
N_NEAR = 3


def place():
    tok, cell = lax.axis_index("tok"), lax.axis_index("cell")
    core = lax.rem(tok, N_CORE)
    z = lax.rem(lax.div(tok, N_CORE), N_Z)
    x = lax.rem(lax.div(tok, N_CORE * N_Z) + lax.rem(cell, N_XH), N_X)

    def z_of(distance):
        return lax.rem(z + distance * (1 - 2 * core) + N_Z, N_Z)

    return x, z_of, core


def block_at(number):
    return pl.ds(pl.multiple_of(number * BLOCK, BLOCK), BLOCK)


def score_near(near, held):
    n_rows, width = held.shape

    def body(near_ref, store_ref, out_ref, rows_ref):
        x, _, _ = place()
        for at, (turn, _) in enumerate(NEAR_BLOCKS):
            x_at = 1 - x if turn else x
            rows_ref[block_at(at // N_X * N_X + x_at), :] = near_ref[at]
        for step in range(n_rows // STEP_ROWS):
            cols = pl.ds(step * STEP_ROWS, STEP_ROWS)
            scores = lax.dot_general(
                rows_ref[...], store_ref[cols, :], NT, preferred_element_type=jnp.float32
            )
            out_ref[:, :, :, cols] = scores.reshape(N_NEAR, N_X, BLOCK, STEP_ROWS)

    vmem = pl.BlockSpec(memory_space=pltpu.VMEM)
    return pl.pallas_call(
        body,
        in_specs=[vmem, vmem],
        out_specs=vmem,
        out_shape=jax.ShapeDtypeStruct((N_NEAR, N_X, BLOCK, n_rows), jnp.float32),
        scratch_shapes=[pltpu.VMEM((len(NEAR_BLOCKS) * BLOCK, width), jnp.bfloat16)],
        compiler_params=pltpu.CompilerParams(vmem_limit_bytes=8 << 20),
    )(near, held)


def score_rest(near_scores, far, near_over, far_over, held):
    n_rows, width = held.shape
    steps = n_rows // STEP_ROWS

    def body(
        near_scores_ref, far_ref, near_over_ref, far_over_ref, store_ref, out_ref,
        rows_ref, far_acc_ref, over_acc_ref, near_sems, sems,
    ):
        x, z_of, core = place()
        copies = []
        for at in range(N_NEAR):
            distance = NEAR_BLOCKS[at * N_X][1]
            copies.append(
                pltpu.make_async_copy(near_scores_ref.at[at], out_ref.at[:, z_of(distance), core], near_sems.at[at])
            )
            copies[-1].start()
        for turn in range(N_X):
            x_at = 1 - x if turn else x
            rows_ref[block_at(x_at), :] = far_ref[turn]
            rows_ref[block_at(N_X + x_at * N_Z + z_of(2)), :] = far_over_ref[turn]
        for at, (turn, distance) in enumerate(NEAR_BLOCKS):
            x_at = 1 - x if turn else x
            rows_ref[block_at(N_X + x_at * N_Z + z_of(-distance)), :] = near_over_ref[at]
        for step in range(steps):
            cols = pl.ds(step * STEP_ROWS, STEP_ROWS)
            scores = lax.dot_general(
                rows_ref[...], store_ref[cols, :], NT, preferred_element_type=jnp.float32
            )
            far_acc_ref[:, :, cols] = scores[: N_X * BLOCK].reshape(N_X, BLOCK, STEP_ROWS)
            over_acc_ref[:, :, :, cols] = scores[N_X * BLOCK :].reshape(N_X, N_Z, BLOCK, STEP_ROWS)
            for at, (source, target) in enumerate((
                (far_acc_ref.at[:, :, cols], out_ref.at[:, z_of(2), core, :, cols]),
                (over_acc_ref.at[:, :, :, cols], out_ref.at[:, :, 1 - core, :, cols]),
            )):
                copies.append(pltpu.make_async_copy(source, target, sems.at[step, at]))
                copies[-1].start()
        for copy in copies:
            copy.wait()

    vmem = pl.BlockSpec(memory_space=pltpu.VMEM)
    return pl.pallas_call(
        body,
        in_specs=[vmem] * 5,
        out_specs=pl.BlockSpec(memory_space=pl.ANY),
        out_shape=jax.ShapeDtypeStruct((N_X, N_Z, N_CORE, BLOCK, n_rows), jnp.float32),
        scratch_shapes=[
            pltpu.VMEM((N_X * (1 + N_Z) * BLOCK, width), jnp.bfloat16),
            pltpu.VMEM((N_X, BLOCK, n_rows), jnp.float32),
            pltpu.VMEM((N_X, N_Z, BLOCK, n_rows), jnp.float32),
            pltpu.SemaphoreType.DMA((N_NEAR,)),
            pltpu.SemaphoreType.DMA((steps, 2)),
        ],
        compiler_params=pltpu.CompilerParams(vmem_limit_bytes=10 << 20),
    )(near_scores, far, near_over, far_over, held)


def hold(stores):
    parts = 4
    size = stores.shape[0] // parts

    def body(store_ref, held_ref, sems):
        copies = []
        for part in range(parts):
            rows = pl.ds(part * size, size)
            copies.append(pltpu.make_async_copy(store_ref.at[rows], held_ref.at[rows], sems.at[part]))
            copies[-1].start()
        for copy in copies:
            copy.wait()

    return pl.pallas_call(
        body,
        in_specs=[pl.BlockSpec(memory_space=pl.ANY)],
        out_specs=pl.BlockSpec(memory_space=pltpu.VMEM),
        out_shape=jax.ShapeDtypeStruct(stores.shape, stores.dtype),
        scratch_shapes=[pltpu.SemaphoreType.DMA((parts,))],
        compiler_params=pltpu.CompilerParams(vmem_limit_bytes=4 << 20),
    )(pltpu.with_memory_space_constraint(stores, pltpu.HBM))


def partial_sums(activations, out_grads, query_ids, live, proj_in, proj_out):
    tok_rows, width = activations.shape
    n_left, n_right = proj_in.shape[1], proj_out.shape[1]
    parts = 2
    arrays = (query_ids.reshape(1, -1), proj_in.T, proj_out.T, out_grads, activations)
    size = tok_rows // parts

    def body(live_ref, *refs):
        small_refs, act_ref, sums_ref = refs[:4], refs[4], refs[5]
        held_refs = refs[6:10]
        rows_ref, left_ref, cells_ref, hot_ref, small_sems, sems = refs[10:]
        small_loads = []
        for at, (source, target) in enumerate(zip(small_refs, held_refs)):
            small_loads.append(pltpu.make_async_copy(source, target, small_sems.at[at]))
            small_loads[-1].start()
        ids_ref, in_ref, out_proj_ref, grad_ref = held_refs
        loads = []
        for part in range(parts):
            rows = pl.ds(part * size, size)
            loads.append(pltpu.make_async_copy(act_ref.at[rows], rows_ref.at[rows], sems.at[part]))
            loads[-1].start()
        small_loads[0].wait()
        swap = lax.rem(lax.axis_index("cell"), N_XH) * (Q // N_X)
        held_at = ids_ref[...] ^ swap
        hit = lax.broadcasted_iota(jnp.int32, (Q, tok_rows), 0) == held_at
        hot_ref[...] = jnp.where(hit, 1.0, 0.0).astype(jnp.bfloat16)
        for load in small_loads[1:]:
            load.wait()
        right = lax.dot_general(out_proj_ref[...], grad_ref[...], NT, preferred_element_type=jnp.float32)
        for part in range(parts):
            loads[part].wait()
            rows = pl.ds(part * size, size)
            left_ref[:, rows] = lax.dot_general(
                in_ref[...], rows_ref[rows, :], NT, preferred_element_type=jnp.float32
            )
        valid = lax.broadcasted_iota(jnp.int32, (1, tok_rows), 1) < live_ref[0]
        mask = jnp.where(valid, 1.0, 0.0)
        for at in range(n_left):
            cells = left_ref[at : at + 1, :] * right * mask
            cells_ref[at * n_right : (at + 1) * n_right, :] = cells.astype(jnp.bfloat16)
        sums = lax.dot_general(hot_ref[...], cells_ref[...], NT, preferred_element_type=jnp.float32)
        sums_ref[...] = sums.astype(jnp.bfloat16)

    vmem = pl.BlockSpec(memory_space=pltpu.VMEM)
    return pl.pallas_call(
        body,
        in_specs=[pl.BlockSpec(memory_space=pltpu.SMEM)] + [pl.BlockSpec(memory_space=pl.ANY)] * 5,
        out_specs=vmem,
        out_shape=jax.ShapeDtypeStruct((Q, n_left * n_right), jnp.bfloat16),
        scratch_shapes=[
            *(pltpu.VMEM(array.shape, array.dtype) for array in arrays[:4]),
            pltpu.VMEM((tok_rows, width), jnp.bfloat16),
            pltpu.VMEM((n_left, tok_rows), jnp.float32),
            pltpu.VMEM((n_left * n_right, tok_rows), jnp.bfloat16),
            pltpu.VMEM((Q, tok_rows), jnp.bfloat16),
            pltpu.SemaphoreType.DMA((4,)),
            pltpu.SemaphoreType.DMA((parts,)),
        ],
        compiler_params=pltpu.CompilerParams(vmem_limit_bytes=24 << 20),
    )(live, *(pltpu.with_memory_space_constraint(array, pltpu.HBM) for array in arrays))


def shards(activations, out_grads, query_ids, live, proj_in, proj_out, whitener, stores):
    partial_value = partial_sums(activations, out_grads, query_ids, live, proj_in, proj_out)
    pieces = lax.all_to_all(partial_value.reshape(N_TOK, BLOCK, -1), "tok", 0, 0, tiled=True)
    summed = pieces.astype(jnp.float32).sum(0).astype(jnp.bfloat16)
    total = jnp.dot(summed, whitener, preferred_element_type=jnp.float32)
    across = send(total.astype(jnp.bfloat16), SUM_X)
    held = hold(stores)
    total = total + across.astype(jnp.float32)
    rounded = total.astype(jnp.bfloat16)
    for piece in [send(rounded, route) for route in SUM_Y]:
        total = total + piece.astype(jnp.float32)
    return gather_and_score(total.astype(jnp.bfloat16), held)


def gather_and_score(own, held):
    here = (own, send(own, SWAP_X))
    up = tuple(send(piece, RING_A) for piece in here)
    down = tuple(send(piece, RING_B) for piece in here)
    far_own = send(up[0], RING_A)
    far_other = send(up[1], RING_A)
    near = jnp.stack([*here, *up, *down])
    near_over = send(near, SWAP_CORE)
    near_scores = score_near(near, held)
    far = jnp.stack([far_own, far_other])
    far_over = send(far, SWAP_CORE)
    return score_rest(near_scores, far, near_over, far_over, held).reshape(Q, -1)


def solution(mesh):
    in_specs = (
        P("tok", None),
        P("tok", None),
        P("tok"),
        P("tok"),
        P(None, "cell"),
        P(),
        P("cell", None),
        P(("tok", "cell"), None),
    )
    out_specs = P(None, ("tok", "cell"))
    return jax.shard_map(shards, mesh=mesh, in_specs=in_specs, out_specs=out_specs, check_vma=False)
```

```python
import jax
import jax.numpy as jnp
from jax import lax
from jax.experimental import pallas as pl
from jax.experimental.pallas import tpu as pltpu
from jax.sharding import PartitionSpec as P

Q = 512
N_X, N_Z, N_CORE, N_Y, N_XH = 2, 4, 2, 4, 2
N_TOK = N_X * N_Z * N_CORE
BLOCK = Q // N_TOK
AXES = ("tok", "cell")
NT = (((1,), (1,)), ((), ()))
STEP_ROWS = 512


PLACES = [
    (x, z, core, y, xh)
    for x in range(N_X)
    for z in range(N_Z)
    for core in range(N_CORE)
    for y in range(N_Y)
    for xh in range(N_XH)
]


def number(x, z, core, y, xh):
    return (((x * N_Z + z % N_Z) * N_CORE + core) * N_Y + y) * N_XH + xh


def routes(move):
    return [(number(*place), number(*move(*place))) for place in PLACES]


SUM_X = routes(lambda x, z, core, y, xh: (1 - x, z, core, y, 1 - xh))
SUM_Y = [
    routes(lambda x, z, core, y, xh, step=step: (x, z, core, (y + step * (1 - 2 * core)) % N_Y, xh)) for step in (1, 3, 2)
]
SWAP_X = routes(lambda x, z, core, y, xh: (1 - x, z, core, y, xh))
SWAP_CORE = routes(lambda x, z, core, y, xh: (x, z, 1 - core, y, xh))
RING_A = routes(lambda x, z, core, y, xh: (x, z + 1 - 2 * core, core, y, xh))
RING_B = routes(lambda x, z, core, y, xh: (x, z - 1 + 2 * core, core, y, xh))


def send(value, route):
    return lax.ppermute(value, AXES, route)


NEAR_BLOCKS = ((0, 0), (1, 0), (0, -1), (1, -1), (0, 1), (1, 1))
N_NEAR = 3


def place():
    tok, cell = lax.axis_index("tok"), lax.axis_index("cell")
    core = lax.rem(tok, N_CORE)
    z = lax.rem(lax.div(tok, N_CORE), N_Z)
    x = lax.rem(lax.div(tok, N_CORE * N_Z) + lax.rem(cell, N_XH), N_X)

    def z_of(distance):
        return lax.rem(z + distance * (1 - 2 * core) + N_Z, N_Z)

    return x, z_of, core


def block_at(number):
    return pl.ds(pl.multiple_of(number * BLOCK, BLOCK), BLOCK)


def score_near(near, held):
    n_rows, width = held.shape

    def body(near_ref, store_ref, out_ref, rows_ref):
        x, _, _ = place()
        for at, (turn, _) in enumerate(NEAR_BLOCKS):
            x_at = 1 - x if turn else x
            rows_ref[block_at(at // N_X * N_X + x_at), :] = near_ref[at]
        for step in range(n_rows // STEP_ROWS):
            cols = pl.ds(step * STEP_ROWS, STEP_ROWS)
            scores = lax.dot_general(
                rows_ref[...], store_ref[cols, :], NT, preferred_element_type=jnp.float32
            )
            out_ref[:, :, :, cols] = scores.reshape(N_NEAR, N_X, BLOCK, STEP_ROWS)

    vmem = pl.BlockSpec(memory_space=pltpu.VMEM)
    return pl.pallas_call(
        body,
        in_specs=[vmem, vmem],
        out_specs=vmem,
        out_shape=jax.ShapeDtypeStruct((N_NEAR, N_X, BLOCK, n_rows), jnp.float32),
        scratch_shapes=[pltpu.VMEM((len(NEAR_BLOCKS) * BLOCK, width), jnp.bfloat16)],
        compiler_params=pltpu.CompilerParams(vmem_limit_bytes=8 << 20),
    )(near, held)


def score_rest(near_scores, far, near_over, far_over, held):
    n_rows, width = held.shape
    steps = n_rows // STEP_ROWS

    def body(
        near_scores_ref, far_0, far_1, near_over_ref, far_over_0, far_over_1, store_ref, out_ref,
        rows_ref, far_acc_ref, over_acc_ref, near_sems, sems,
    ):
        x, z_of, core = place()
        copies = []
        for at in range(N_NEAR):
            distance = NEAR_BLOCKS[at * N_X][1]
            copies.append(
                pltpu.make_async_copy(near_scores_ref.at[at], out_ref.at[:, z_of(distance), core], near_sems.at[at])
            )
            copies[-1].start()
        for turn in range(N_X):
            x_at = 1 - x if turn else x
            rows_ref[block_at(x_at), :] = (far_0, far_1)[turn][...]
            rows_ref[block_at(N_X + x_at * N_Z + z_of(2)), :] = (far_over_0, far_over_1)[turn][...]
        for at, (turn, distance) in enumerate(NEAR_BLOCKS):
            x_at = 1 - x if turn else x
            rows_ref[block_at(N_X + x_at * N_Z + z_of(-distance)), :] = near_over_ref[at]
        for step in range(steps):
            cols = pl.ds(step * STEP_ROWS, STEP_ROWS)
            scores = lax.dot_general(
                rows_ref[...], store_ref[cols, :], NT, preferred_element_type=jnp.float32
            )
            far_acc_ref[:, :, cols] = scores[: N_X * BLOCK].reshape(N_X, BLOCK, STEP_ROWS)
            over_acc_ref[:, :, :, cols] = scores[N_X * BLOCK :].reshape(N_X, N_Z, BLOCK, STEP_ROWS)
            for at, (source, target) in enumerate((
                (far_acc_ref.at[:, :, cols], out_ref.at[:, z_of(2), core, :, cols]),
                (over_acc_ref.at[:, :, :, cols], out_ref.at[:, :, 1 - core, :, cols]),
            )):
                copies.append(pltpu.make_async_copy(source, target, sems.at[step, at]))
                copies[-1].start()
        for copy in copies:
            copy.wait()

    vmem = pl.BlockSpec(memory_space=pltpu.VMEM)
    return pl.pallas_call(
        body,
        in_specs=[vmem] * 7,
        out_specs=pl.BlockSpec(memory_space=pl.ANY),
        out_shape=jax.ShapeDtypeStruct((N_X, N_Z, N_CORE, BLOCK, n_rows), jnp.float32),
        scratch_shapes=[
            pltpu.VMEM((N_X * (1 + N_Z) * BLOCK, width), jnp.bfloat16),
            pltpu.VMEM((N_X, BLOCK, n_rows), jnp.float32),
            pltpu.VMEM((N_X, N_Z, BLOCK, n_rows), jnp.float32),
            pltpu.SemaphoreType.DMA((N_NEAR,)),
            pltpu.SemaphoreType.DMA((steps, 2)),
        ],
        compiler_params=pltpu.CompilerParams(vmem_limit_bytes=10 << 20),
    )(near_scores, *far, near_over, *far_over, held)


def hold(stores):
    parts = 4
    size = stores.shape[0] // parts

    def body(store_ref, held_ref, sems):
        copies = []
        for part in range(parts):
            rows = pl.ds(part * size, size)
            copies.append(pltpu.make_async_copy(store_ref.at[rows], held_ref.at[rows], sems.at[part]))
            copies[-1].start()
        for copy in copies:
            copy.wait()

    return pl.pallas_call(
        body,
        in_specs=[pl.BlockSpec(memory_space=pl.ANY)],
        out_specs=pl.BlockSpec(memory_space=pltpu.VMEM),
        out_shape=jax.ShapeDtypeStruct(stores.shape, stores.dtype),
        scratch_shapes=[pltpu.SemaphoreType.DMA((parts,))],
        compiler_params=pltpu.CompilerParams(vmem_limit_bytes=4 << 20),
    )(pltpu.with_memory_space_constraint(stores, pltpu.HBM))


def partial_sums(activations, out_grads, query_ids, live, proj_in, proj_out):
    tok_rows, width = activations.shape
    n_left, n_right = proj_in.shape[1], proj_out.shape[1]
    parts = 2
    arrays = (query_ids.reshape(1, -1), proj_in.T, proj_out.T, out_grads, activations)
    size = tok_rows // parts

    def body(live_ref, *refs):
        small_refs, act_ref, sums_ref = refs[:4], refs[4], refs[5]
        held_refs = refs[6:10]
        rows_ref, left_ref, cells_ref, hot_ref, small_sems, sems = refs[10:]
        small_loads = []
        for at, (source, target) in enumerate(zip(small_refs, held_refs)):
            small_loads.append(pltpu.make_async_copy(source, target, small_sems.at[at]))
            small_loads[-1].start()
        ids_ref, in_ref, out_proj_ref, grad_ref = held_refs
        loads = []
        for part in range(parts):
            rows = pl.ds(part * size, size)
            loads.append(pltpu.make_async_copy(act_ref.at[rows], rows_ref.at[rows], sems.at[part]))
            loads[-1].start()
        small_loads[0].wait()
        swap = lax.rem(lax.axis_index("cell"), N_XH) * (Q // N_X)
        held_at = ids_ref[...] ^ swap
        hit = lax.broadcasted_iota(jnp.int32, (Q, tok_rows), 0) == held_at
        hot_ref[...] = jnp.where(hit, 1.0, 0.0).astype(jnp.bfloat16)
        for load in small_loads[1:]:
            load.wait()
        right = lax.dot_general(out_proj_ref[...], grad_ref[...], NT, preferred_element_type=jnp.float32)
        for part in range(parts):
            loads[part].wait()
            rows = pl.ds(part * size, size)
            left_ref[:, rows] = lax.dot_general(
                in_ref[...], rows_ref[rows, :], NT, preferred_element_type=jnp.float32
            )
        valid = lax.broadcasted_iota(jnp.int32, (1, tok_rows), 1) < live_ref[0]
        mask = jnp.where(valid, 1.0, 0.0)
        for at in range(n_left):
            cells = left_ref[at : at + 1, :] * right * mask
            cells_ref[at * n_right : (at + 1) * n_right, :] = cells.astype(jnp.bfloat16)
        sums = lax.dot_general(hot_ref[...], cells_ref[...], NT, preferred_element_type=jnp.float32)
        sums_ref[...] = sums.astype(jnp.bfloat16)

    vmem = pl.BlockSpec(memory_space=pltpu.VMEM)
    return pl.pallas_call(
        body,
        in_specs=[pl.BlockSpec(memory_space=pltpu.SMEM)] + [pl.BlockSpec(memory_space=pl.ANY)] * 5,
        out_specs=vmem,
        out_shape=jax.ShapeDtypeStruct((Q, n_left * n_right), jnp.bfloat16),
        scratch_shapes=[
            *(pltpu.VMEM(array.shape, array.dtype) for array in arrays[:4]),
            pltpu.VMEM((tok_rows, width), jnp.bfloat16),
            pltpu.VMEM((n_left, tok_rows), jnp.float32),
            pltpu.VMEM((n_left * n_right, tok_rows), jnp.bfloat16),
            pltpu.VMEM((Q, tok_rows), jnp.bfloat16),
            pltpu.SemaphoreType.DMA((4,)),
            pltpu.SemaphoreType.DMA((parts,)),
        ],
        compiler_params=pltpu.CompilerParams(vmem_limit_bytes=24 << 20),
    )(live, *(pltpu.with_memory_space_constraint(array, pltpu.HBM) for array in arrays))


def shards(activations, out_grads, query_ids, live, proj_in, proj_out, whitener, stores):
    partial_value = partial_sums(activations, out_grads, query_ids, live, proj_in, proj_out)
    pieces = lax.all_to_all(partial_value.reshape(N_TOK, BLOCK, -1), "tok", 0, 0, tiled=True)
    summed = pieces.astype(jnp.float32).sum(0).astype(jnp.bfloat16)
    total = jnp.dot(summed, whitener, preferred_element_type=jnp.float32)
    across = send(total.astype(jnp.bfloat16), SUM_X)
    held = hold(stores)
    total = total + across.astype(jnp.float32)
    rounded = total.astype(jnp.bfloat16)
    for piece in [send(rounded, route) for route in SUM_Y]:
        total = total + piece.astype(jnp.float32)
    return gather_and_score(total.astype(jnp.bfloat16), held)


def gather_and_score(own, held):
    here = (own, send(own, SWAP_X))
    up = tuple(send(piece, RING_A) for piece in here)
    down = tuple(send(piece, RING_B) for piece in here)
    far_own = send(up[0], RING_A)
    far_other = send(up[1], RING_A)
    near = jnp.stack([*here, *up, *down])
    near_over = send(near, SWAP_CORE)
    near_scores = score_near(near, held)
    far = (far_own, far_other)
    far_over = tuple(send(piece, SWAP_CORE) for piece in far)
    return score_rest(near_scores, far, near_over, far_over, held).reshape(Q, -1)


def solution(mesh):
    in_specs = (
        P("tok", None),
        P("tok", None),
        P("tok"),
        P("tok"),
        P(None, "cell"),
        P(),
        P("cell", None),
        P(("tok", "cell"), None),
    )
    out_specs = P(None, ("tok", "cell"))
    return jax.shard_map(shards, mesh=mesh, in_specs=in_specs, out_specs=out_specs, check_vma=False)
```
